32 devices in a mesh: clip: 16 (over z, x, core), seq: 2 (over y).
Axes of the slice: x: 2, y: 2, z: 4, core: 2. Of those that a mesh axis runs over, the one named last changes fastest.
Arguments:
- inputs: bfloat16 [32, 128, 768], P('clip', 'seq'), may hold values from -6 to 6
- micro_live: int32 [32], P('clip'), may hold values from 0 to 1, as said below
- ln1_gain: bfloat16 [768], P(('clip', 'seq')), may hold values from 0.099609375 to 1.8984375
- ln1_shift: bfloat16 [768], P(('clip', 'seq')), may hold values from -3 to 3
- w_q: bfloat16 [768, 768], P(('clip', 'seq')), may hold values from -0.21875 to 0.21875
- b_q: bfloat16 [768], P(('clip', 'seq')), may hold values from -4 to 4
- w_k: bfloat16 [768, 768], P(('clip', 'seq')), may hold values from -0.21875 to 0.21875
- w_v: bfloat16 [768, 768], P(('clip', 'seq')), may hold values from -0.21875 to 0.21875
- b_v: bfloat16 [768], P(('clip', 'seq')), may hold values from -3 to 3
- w_o: bfloat16 [768, 768], P(('clip', 'seq')), may hold values from -0.4375 to 0.4375
- b_o: bfloat16 [768], P(('clip', 'seq')), may hold values from -3 to 3
- ln2_gain: bfloat16 [768], P(('clip', 'seq')), may hold values from 0.099609375 to 1.8984375
- ln2_shift: bfloat16 [768], P(('clip', 'seq')), may hold values from -3 to 3
- w_fc1: bfloat16 [768, 3072], P(('clip', 'seq')), may hold values from -0.21875 to 0.21875
- b_fc1: bfloat16 [3072], P(('clip', 'seq')), may hold values from -3 to 3
- w_fc2: bfloat16 [3072, 768], P(('clip', 'seq')), may hold values from -0.109375 to 0.109375
- b_fc2: bfloat16 [768], P(('clip', 'seq')), may hold values from -3 to 3
- grad_out: bfloat16 [32, 128, 768], P('clip', 'seq'), may hold values from -6 to 6
Outputs:
- out_rows: bfloat16 [32, 128, 768], P('clip', 'seq')
- grad_rows: float32 [32, 128, 768], P('clip', 'seq')
- grad_ln1_gain: float32 [768], P(('clip', 'seq'))
- grad_ln1_shift: float32 [768], P(('clip', 'seq'))
- grad_w_q: float32 [768, 768], P(('clip', 'seq'))
- grad_b_q: float32 [768], P(('clip', 'seq'))
- grad_w_k: float32 [768, 768], P(('clip', 'seq'))
- grad_w_v: float32 [768, 768], P(('clip', 'seq'))
- grad_b_v: float32 [768], P(('clip', 'seq'))
- grad_w_o: float32 [768, 768], P(('clip', 'seq'))
- grad_b_o: float32 [768], P(('clip', 'seq'))
- grad_ln2_gain: float32 [768], P(('clip', 'seq'))
- grad_ln2_shift: float32 [768], P(('clip', 'seq'))
- grad_w_fc1: float32 [768, 3072], P(('clip', 'seq'))
- grad_b_fc1: float32 [3072], P(('clip', 'seq'))
- grad_w_fc2: float32 [3072, 768], P(('clip', 'seq'))
- grad_b_fc2: float32 [768], P(('clip', 'seq'))
The draws below stay inside these ranges and needn't reach their ends.
Inputs may be any that keep to these rules, and one draw needn't show every extreme that they name: `micro_live`: entry 2 * g + m is 1 where micro-batch slot m of clip group g holds a clip, else 0. Slot 0 of every group holds a clip; in every draw some group has all 2 slots filled.
All inputs are finite; a program needn't handle non-finite values.
Results may differ from the reference program's by a relative error of at most 0.013.
Values may be sent and summed in bfloat16 or wider, within the bound.
No kernel may reach another device: no remote copies, remote signals or barrier semaphores. Data moves between devices by JAX's collectives and lax.ppermute only.
A program may use at most 192 MiB of HBM per device.

```python
import math
import jax
import jax.numpy as jnp
from jax import lax

D = 768
HEADS = 12
HD = 64
FF = 3072
MB = 2
L = 128
SLOTS = 32


def draw_micro_live(key, part):
    groups = SLOTS // MB
    first, second = jax.random.split(jax.random.fold_in(key, 11))
    table = jax.random.randint(first, (groups, MB), 0, 2)
    busy = jax.random.randint(second, (), 0, groups)
    group_ids = jnp.arange(groups)[:, None]
    slot_ids = jnp.arange(MB)[None, :]
    table = jnp.where(slot_ids == 0, 1, table)
    table = jnp.where(group_ids == busy, 1, table)
    return table.reshape(-1).astype(jnp.int32)


def shard_levels(own_key, extent, cuts, least, top_value):
    def one(dim, blocks):
        steps = jax.random.uniform(jax.random.fold_in(jax.random.fold_in(own_key, 6), dim), (blocks,), jnp.float32, least / len(cuts), top_value / len(cuts))
        return jnp.repeat(jnp.exp(steps), extent[dim] // blocks).reshape((-1,) + (1,) * (len(extent) - dim - 1))

    loudness = one(*cuts[0])
    for cut in cuts[1:]:
        loudness = loudness * one(*cut)
    return loudness


def gaussian(own_key, extent, scale, reach, cuts=(), held_as=jnp.bfloat16):
    values = scale * jax.random.normal(own_key, extent, jnp.float32)
    if cuts:
        values = values * shard_levels(own_key, extent, cuts, -0.22, 0.18)
    return jnp.clip(values, -reach, reach).astype(held_as)


def setup_inputs(seed: int = 0) -> dict:
    key_of = jax.random.split(jax.random.key(seed), 19)
    return {
        "inputs": gaussian(key_of[0], (SLOTS, L, D), 1.0, 6.0, ((0, 16), (1, 2))),
        "micro_live": draw_micro_live(jax.random.fold_in(key_of[18], 71), 0),
        "ln1_gain": jnp.clip(1.0 + 0.18 * jax.random.normal(key_of[2], (D,), jnp.float32), 0.099609375, 1.8984375).astype(jnp.bfloat16),
        "ln1_shift": gaussian(key_of[3], (D,), 0.5, 3.0, ((0, 32),)),
        "w_q": gaussian(key_of[4], (D, D), D ** -0.5, 0.21875, ((0, 32),)),
        "b_q": gaussian(key_of[5], (D,), 1.0, 4.0, ((0, 32),)),
        "w_k": gaussian(key_of[6], (D, D), D ** -0.5, 0.21875, ((0, 32),)),
        "w_v": gaussian(key_of[7], (D, D), D ** -0.5, 0.21875, ((0, 32),)),
        "b_v": gaussian(key_of[8], (D,), 0.5, 3.0, ((0, 32),)),
        "w_o": gaussian(key_of[9], (D, D), (max(D * 32 // L, 8)) ** -0.5, 0.4375, ((0, 32),)),
        "b_o": gaussian(key_of[10], (D,), 0.5, 3.0, ((0, 32),)),
        "ln2_gain": jnp.clip(1.0 + 0.18 * jax.random.normal(key_of[11], (D,), jnp.float32), 0.099609375, 1.8984375).astype(jnp.bfloat16),
        "ln2_shift": gaussian(key_of[12], (D,), 0.5, 3.0, ((0, 32),)),
        "w_fc1": gaussian(key_of[13], (D, FF), D ** -0.5, 0.21875, ((0, 32),)),
        "b_fc1": gaussian(key_of[14], (FF,), 0.5, 3.0, ((0, 32),)),
        "w_fc2": gaussian(key_of[15], (FF, D), FF ** -0.5, 0.109375, ((0, 32),)),
        "b_fc2": gaussian(key_of[16], (D,), 0.5, 3.0, ((0, 32),)),
        "grad_out": gaussian(key_of[17], (SLOTS, L, D), 1.0, 6.0, ((0, 16), (1, 2))),
    }


norm_eps = 1e-05

def layer_norm(values, gain, shift):
    center = values - lax.optimization_barrier(jnp.mean(values, axis=-1, keepdims=True))
    inv_std = lax.rsqrt(lax.optimization_barrier(jnp.mean(center * center, axis=-1, keepdims=True)) + norm_eps)
    normed = center * inv_std
    return (normed * gain + shift, normed, inv_std)

def norm_back(grad_in, normed, inv_std, gain):
    scaled = grad_in * gain
    inner = scaled - lax.optimization_barrier(jnp.mean(scaled, axis=-1, keepdims=True)) - normed * lax.optimization_barrier(jnp.mean(scaled * normed, axis=-1, keepdims=True))
    return inv_std * inner

def gelu_slope(pre):
    return 0.5 * (1.0 + lax.erf(pre * 0.7071067811865476)) + pre * jnp.exp(-0.5 * pre * pre) * 0.3989422804014327

def tdot(left, right):
    return jnp.dot(left, right, preferred_element_type=jnp.float32)

def slot_pass(params, rows, live_flag, cotangent):
    g1, c1, wq, bq, wk, wv, bv, wo, bo, g2, c2, wf1, bf1, wf2, bf2 = params
    f32 = jnp.float32
    bf16 = jnp.bfloat16
    scale = 1.0 / math.sqrt(HD)
    count = rows.shape[0]
    x = rows.astype(f32)
    h1, n1, r1 = layer_norm(x, g1.astype(f32), c1.astype(f32))
    h1b = h1.astype(bf16)
    qb = (tdot(h1b, wq) + bq.astype(f32)).astype(bf16)
    kb = tdot(h1b, wk).astype(bf16)
    vb = (tdot(h1b, wv) + bv.astype(f32)).astype(bf16)
    q3 = qb.reshape(count, HEADS, HD).astype(f32)
    k3 = kb.reshape(count, HEADS, HD).astype(f32)
    v3 = vb.reshape(count, HEADS, HD).astype(f32)
    scores = jnp.einsum('qhd,khd->hqk', q3, k3) * scale
    peak = lax.optimization_barrier(jnp.max(scores, axis=-1, keepdims=True))
    lse = peak + jnp.log(lax.optimization_barrier(jnp.sum(jnp.exp(scores - peak), axis=-1, keepdims=True)))
    probs = jnp.exp(scores - lse)
    pb = probs.astype(bf16)
    ctxb = jnp.einsum('hqk,khd->qhd', pb.astype(f32), v3).reshape(count, D).astype(bf16)
    mid = x + tdot(ctxb, wo) + bo.astype(f32)
    h2, n2, r2 = layer_norm(mid, g2.astype(f32), c2.astype(f32))
    h2b = h2.astype(bf16)
    pre = tdot(h2b, wf1) + bf1.astype(f32)
    actb = jax.nn.gelu(pre, approximate=False).astype(bf16)
    result = (live_flag * (mid + tdot(actb, wf2) + bf2.astype(f32))).astype(bf16)
    gy = live_flag * cotangent.astype(f32)
    gyb = gy.astype(bf16)
    dpre = tdot(gyb, wf2.T) * gelu_slope(pre)
    dpreb = dpre.astype(bf16)
    dh2 = tdot(dpreb, wf1.T)
    dmid = gy + norm_back(dh2, n2, r2, g2.astype(f32))
    dmidb = dmid.astype(bf16)
    dctxb = tdot(dmidb, wo.T).astype(bf16)
    dc3 = dctxb.reshape(count, HEADS, HD).astype(f32)
    dprob = jnp.einsum('qhd,khd->hqk', dc3, v3)
    delta = lax.optimization_barrier(jnp.sum(probs * dprob, axis=-1, keepdims=True))
    dsb = (probs * (dprob - delta) * scale).astype(bf16).astype(f32)
    dq = jnp.einsum('hqk,khd->qhd', dsb, k3).reshape(count, D)
    dk = jnp.einsum('hqk,qhd->khd', dsb, q3).reshape(count, D)
    dv = jnp.einsum('hqk,qhd->khd', pb.astype(f32), dc3).reshape(count, D)
    dqb = dq.astype(bf16)
    dkb = dk.astype(bf16)
    dvb = dv.astype(bf16)
    dh1 = tdot(dqb, wq.T) + tdot(dkb, wk.T) + tdot(dvb, wv.T)
    grad_x = dmid + norm_back(dh1, n1, r1, g1.astype(f32))
    grads = (lax.optimization_barrier(jnp.sum(dh1 * n1, axis=0)), lax.optimization_barrier(jnp.sum(dh1, axis=0)), tdot(h1b.T, dqb), lax.optimization_barrier(jnp.sum(dq, axis=0)), tdot(h1b.T, dkb), tdot(h1b.T, dvb), lax.optimization_barrier(jnp.sum(dv, axis=0)), tdot(ctxb.T, dmidb), lax.optimization_barrier(jnp.sum(dmid, axis=0)), lax.optimization_barrier(jnp.sum(dh2 * n2, axis=0)), lax.optimization_barrier(jnp.sum(dh2, axis=0)), tdot(h2b.T, dpreb), lax.optimization_barrier(jnp.sum(dpre, axis=0)), tdot(actb.T, gyb), lax.optimization_barrier(jnp.sum(gy, axis=0)))
    return (result, grad_x, grads)

def reference(inputs, micro_live, ln1_gain, ln1_shift, w_q, b_q, w_k, w_v, b_v, w_o, b_o, ln2_gain, ln2_shift, w_fc1, b_fc1, w_fc2, b_fc2, grad_out):
    params = (ln1_gain, ln1_shift, w_q, b_q, w_k, w_v, b_v, w_o, b_o, ln2_gain, ln2_shift, w_fc1, b_fc1, w_fc2, b_fc2)
    zeros = tuple((jnp.zeros(p.shape, jnp.float32) for p in params))

    def one_slot(carry, item):
        rows, flag, cotangent = item
        result, grad_x, grads = slot_pass(params, rows, flag.astype(jnp.float32), cotangent)
        return (tuple((a + b for a, b in zip(carry, grads))), (result, grad_x))
    totals, (out_rows, grad_rows) = lax.scan(one_slot, zeros, (inputs, micro_live, grad_out))
    return (out_rows, grad_rows, totals[0], totals[1], totals[2], totals[3], totals[4], totals[5], totals[6], totals[7], totals[8], totals[9], totals[10], totals[11], totals[12], totals[13], totals[14])
```

```python
import functools
import math

import jax
import jax.numpy as jnp
from jax import lax
from jax.experimental import pallas as pl
from jax.experimental.pallas import tpu as pltpu
from jax.sharding import Mesh
from jax.sharding import PartitionSpec as P

HEADS = 12
HD = 64


norm_eps = 1e-05


def layer_norm(values, gain, shift):
    center = values - jnp.mean(values, axis=-1, keepdims=True)
    inv_std = lax.rsqrt(jnp.mean(center * center, axis=-1, keepdims=True) + norm_eps)
    normed = center * inv_std
    return (normed * gain + shift, normed, inv_std)


def norm_back(grad_in, normed, inv_std, gain):
    scaled = grad_in * gain
    inner = (
        scaled
        - jnp.mean(scaled, axis=-1, keepdims=True)
        - normed * jnp.mean(scaled * normed, axis=-1, keepdims=True)
    )
    return inv_std * inner


def gelu_slope(pre):
    return (
        0.5 * (1.0 + lax.erf(pre * 0.7071067811865476))
        + pre * jnp.exp(-0.5 * pre * pre) * 0.3989422804014327
    )


def tdot(left, right):
    return jnp.dot(left, right, preferred_element_type=jnp.float32)


def on_device_gathered(
    inputs,
    micro_live,
    ln1_gain,
    ln1_shift,
    w_q,
    b_q,
    w_k,
    w_v,
    b_v,
    w_o,
    b_o,
    ln2_gain,
    ln2_shift,
    w_fc1,
    b_fc1,
    w_fc2,
    b_fc2,
    grad_out,
):
    f32 = jnp.float32
    bf16 = jnp.bfloat16
    scale = 1.0 / math.sqrt(HD)
    params = (
        lax.all_gather(ln1_gain, ("clip", "seq"), axis=0, tiled=True),
        lax.all_gather(ln1_shift, ("clip", "seq"), axis=0, tiled=True),
        lax.all_gather(w_q, ("clip", "seq"), axis=0, tiled=True),
        lax.all_gather(b_q, ("clip", "seq"), axis=0, tiled=True),
        lax.all_gather(w_k, ("clip", "seq"), axis=0, tiled=True),
        lax.all_gather(w_v, ("clip", "seq"), axis=0, tiled=True),
        lax.all_gather(b_v, ("clip", "seq"), axis=0, tiled=True),
        lax.all_gather(w_o, ("clip", "seq"), axis=0, tiled=True),
        lax.all_gather(b_o, ("clip", "seq"), axis=0, tiled=True),
        lax.all_gather(ln2_gain, ("clip", "seq"), axis=0, tiled=True),
        lax.all_gather(ln2_shift, ("clip", "seq"), axis=0, tiled=True),
        lax.all_gather(w_fc1, ("clip", "seq"), axis=0, tiled=True),
        lax.all_gather(b_fc1, ("clip", "seq"), axis=0, tiled=True),
        lax.all_gather(w_fc2, ("clip", "seq"), axis=0, tiled=True),
        lax.all_gather(b_fc2, ("clip", "seq"), axis=0, tiled=True),
    )
    g1, c1, wq, bq, wk, wv, bv, wo, bo, g2, c2, wf1, bf1, wf2, bf2 = params
    slots, count, width = inputs.shape
    total_rows = slots * count
    live = micro_live.astype(f32)[:, None, None]
    x = inputs.astype(f32)
    h1, n1, r1 = layer_norm(x, g1.astype(f32), c1.astype(f32))
    h1b = h1.astype(bf16).reshape(total_rows, width)
    qb = (tdot(h1b, wq) + bq.astype(f32)).astype(bf16).reshape(slots, count, width)
    kb = tdot(h1b, wk).astype(bf16).reshape(slots, count, width)
    vb = (tdot(h1b, wv) + bv.astype(f32)).astype(bf16).reshape(slots, count, width)
    key_all, value_all = (
        lax.all_gather(kb, "seq", axis=1, tiled=True),
        lax.all_gather(vb, "seq", axis=1, tiled=True),
    )
    frames = key_all.shape[1]
    q4 = qb.reshape(slots, count, HEADS, HD)
    k4 = key_all.reshape(slots, frames, HEADS, HD)
    v4 = value_all.reshape(slots, frames, HEADS, HD)
    scores = jnp.einsum("sqhd,skhd->shqk", q4, k4, preferred_element_type=f32) * scale
    peak = jnp.max(scores, axis=-1, keepdims=True)
    lse = peak + jnp.log(jnp.sum(jnp.exp(scores - peak), axis=-1, keepdims=True))
    probs = jnp.exp(scores - lse)
    pb = probs.astype(bf16)
    ctxb = (
        jnp.einsum("shqk,skhd->sqhd", pb, v4, preferred_element_type=f32)
        .reshape(total_rows, width)
        .astype(bf16)
    )
    mid = x + tdot(ctxb, wo).reshape(slots, count, width) + bo.astype(f32)
    h2, n2, r2 = layer_norm(mid, g2.astype(f32), c2.astype(f32))
    h2b = h2.astype(bf16).reshape(total_rows, width)
    pre = tdot(h2b, wf1) + bf1.astype(f32)
    actb = jax.nn.gelu(pre, approximate=False).astype(bf16)
    result = (live * (mid + tdot(actb, wf2).reshape(slots, count, width) + bf2.astype(f32))).astype(
        bf16
    )
    gy = live * grad_out.astype(f32)
    gyb = gy.astype(bf16).reshape(total_rows, width)
    dpre = tdot(gyb, wf2.T) * gelu_slope(pre)
    dpreb = dpre.astype(bf16)
    dh2 = tdot(dpreb, wf1.T).reshape(slots, count, width)
    dmid = gy + norm_back(dh2, n2, r2, g2.astype(f32))
    dmidb = dmid.astype(bf16).reshape(total_rows, width)
    dctxb = tdot(dmidb, wo.T).astype(bf16).reshape(slots, count, width)
    dc4 = dctxb.reshape(slots, count, HEADS, HD)
    dprob = jnp.einsum("sqhd,skhd->shqk", dc4, v4, preferred_element_type=f32)
    delta = jnp.sum(probs * dprob, axis=-1, keepdims=True)
    dsb = (probs * (dprob - delta) * scale).astype(bf16)
    dq = jnp.einsum("shqk,skhd->sqhd", dsb, k4, preferred_element_type=f32).reshape(
        total_rows, width
    )
    key_terms = jnp.einsum("shqk,sqhd->skhd", dsb, q4, preferred_element_type=f32).reshape(
        slots, frames, width
    )
    value_terms = jnp.einsum("shqk,sqhd->skhd", pb, dc4, preferred_element_type=f32).reshape(
        slots, frames, width
    )
    dk, dv = (
        lax.psum_scatter(key_terms, "seq", scatter_dimension=1, tiled=True),
        lax.psum_scatter(value_terms, "seq", scatter_dimension=1, tiled=True),
    )
    dk = dk.reshape(total_rows, width)
    dv = dv.reshape(total_rows, width)
    dqb = dq.astype(bf16)
    dkb = dk.astype(bf16)
    dvb = dv.astype(bf16)
    dh1 = (tdot(dqb, wq.T) + tdot(dkb, wk.T) + tdot(dvb, wv.T)).reshape(slots, count, width)
    grad_x = dmid + norm_back(dh1, n1, r1, g1.astype(f32))
    first_cols = h1b.T
    ctx_cols = ctxb.T
    second_cols = h2b.T
    stacked = lax.psum_scatter(
        jnp.concatenate(
            [
                tdot(first_cols, dqb),
                tdot(first_cols, dkb),
                tdot(first_cols, dvb),
                tdot(ctx_cols, dmidb),
                tdot(second_cols, dpreb),
            ],
            axis=1,
        ),
        ("clip", "seq"),
        scatter_dimension=0,
        tiled=True,
    )
    act_cols = actb.T
    grad_fc2 = lax.psum_scatter(
        tdot(act_cols, gyb), ("clip", "seq"), scatter_dimension=0, tiled=True
    )
    grad_q = stacked[:, 0:width]
    grad_k = stacked[:, width : 2 * width]
    grad_v = stacked[:, 2 * width : 3 * width]
    grad_o = stacked[:, 3 * width : 4 * width]
    grad_fc1 = stacked[:, 4 * width :]
    n1f = n1.reshape(total_rows, width)
    n2f = n2.reshape(total_rows, width)
    dh1f = dh1.reshape(total_rows, width)
    dh2f = dh2.reshape(total_rows, width)
    dmidf = dmid.reshape(total_rows, width)
    gyf = gy.reshape(total_rows, width)
    vectors = (
        lax.psum_scatter(
            jnp.sum(dh1f * n1f, axis=0), ("clip", "seq"), scatter_dimension=0, tiled=True
        ),
        lax.psum_scatter(jnp.sum(dh1f, axis=0), ("clip", "seq"), scatter_dimension=0, tiled=True),
        lax.psum_scatter(jnp.sum(dq, axis=0), ("clip", "seq"), scatter_dimension=0, tiled=True),
        lax.psum_scatter(jnp.sum(dv, axis=0), ("clip", "seq"), scatter_dimension=0, tiled=True),
        lax.psum_scatter(jnp.sum(dmidf, axis=0), ("clip", "seq"), scatter_dimension=0, tiled=True),
        lax.psum_scatter(
            jnp.sum(dh2f * n2f, axis=0), ("clip", "seq"), scatter_dimension=0, tiled=True
        ),
        lax.psum_scatter(jnp.sum(dh2f, axis=0), ("clip", "seq"), scatter_dimension=0, tiled=True),
        lax.psum_scatter(jnp.sum(dpre, axis=0), ("clip", "seq"), scatter_dimension=0, tiled=True),
        lax.psum_scatter(jnp.sum(gyf, axis=0), ("clip", "seq"), scatter_dimension=0, tiled=True),
    )
    return (
        result,
        grad_x,
        vectors[0],
        vectors[1],
        grad_q,
        vectors[2],
        grad_k,
        grad_v,
        vectors[3],
        grad_o,
        vectors[4],
        vectors[5],
        vectors[6],
        grad_fc1,
        vectors[7],
        grad_fc2,
        vectors[8],
    )


F32 = jnp.float32
BF16 = jnp.bfloat16
SCALE = 1.0 / math.sqrt(HD)
SWAP = ((0, 1), (1, 0))
VMEM_LIMIT = 56 * 1024 * 1024


def nt_dot(left, right):
    return lax.dot_general(left, right, (((1,), (1,)), ((), ())), preferred_element_type=F32)


def tn_dot(left, right):
    return lax.dot_general(left, right, (((0,), (0,)), ((), ())), preferred_element_type=F32)


def head_masks(rows, width, dtype):
    lanes = lax.broadcasted_iota(jnp.int32, (rows, width), 1)
    return [
        jnp.where((lanes >= h * HD) & (lanes < (h + 1) * HD), 1.0, 0.0).astype(F32).astype(dtype)
        for h in range(width // HD)
    ]


def attention_forward(slots, x, gain, shift, weight, bias):
    part = weight.shape[1] // 3
    frames = x.shape[0] // slots
    h1, _, _ = layer_norm(x.astype(F32), gain, shift)
    h1b = h1.astype(BF16)
    qkv = (tdot(h1b, weight) + bias).astype(BF16)
    q, k, v = qkv[:, :part], qkv[:, part : 2 * part], qkv[:, 2 * part :]
    masks = head_masks(frames, part, BF16)
    masks32 = head_masks(frames, part, F32)
    ctx_rows, all_probs = [], []
    for s in range(slots):
        rows = slice(s * frames, (s + 1) * frames)
        qs, ks, vs = q[rows], k[rows], v[rows]
        ctx = None
        for mask, mask32 in zip(masks, masks32):
            scores = nt_dot(qs * mask, ks) * SCALE
            peak = jnp.max(scores, axis=-1, keepdims=True)
            lse = peak + jnp.log(jnp.sum(jnp.exp(scores - peak), axis=-1, keepdims=True))
            probs = jnp.exp(scores - lse)
            all_probs.append(probs)
            term = tdot(probs.astype(BF16), vs) * mask32
            ctx = term if ctx is None else ctx + term
        ctx_rows.append(ctx)
    ctxb = jnp.concatenate(ctx_rows, axis=0).astype(BF16)
    return h1b, q, k, v, jnp.stack(all_probs), ctxb


def attention_backward(slots, dctx, q, k, v, probs, weight):
    part = q.shape[1]
    frames = q.shape[0] // slots
    masks = head_masks(frames, part, BF16)
    masks32 = head_masks(frames, part, F32)
    dqs, dks, dvs = [], [], []
    for s in range(slots):
        rows = slice(s * frames, (s + 1) * frames)
        ds_, qs, ks, vs = dctx[rows], q[rows], k[rows], v[rows]
        dq = dk = dv = None
        for h, (mask, mask32) in enumerate(zip(masks, masks32)):
            p = probs[s * len(masks) + h]
            dprob = nt_dot(ds_ * mask, vs)
            delta = jnp.sum(p * dprob, axis=-1, keepdims=True)
            dsb = (p * (dprob - delta) * SCALE).astype(BF16)
            tq = tdot(dsb, ks) * mask32
            tk = tn_dot(dsb, qs) * mask32
            tv = tn_dot(p.astype(BF16), ds_) * mask32
            dq = tq if dq is None else dq + tq
            dk = tk if dk is None else dk + tk
            dv = tv if dv is None else dv + tv
        dqs.append(dq)
        dks.append(dk)
        dvs.append(dv)
    dq = jnp.concatenate(dqs, axis=0)
    dk = jnp.concatenate(dks, axis=0)
    dv = jnp.concatenate(dvs, axis=0)
    grads = jnp.concatenate([dq, dk, dv], axis=1).astype(BF16)
    dh1 = nt_dot(grads, weight).astype(BF16)
    return (
        grads,
        dh1,
        jnp.sum(dq, axis=0, keepdims=True)[None],
        jnp.sum(dv, axis=0, keepdims=True)[None],
    )


def out_projection(x, ctx, weight, bias, gain, shift):
    mid = x.astype(F32) + tdot(ctx, weight) + bias
    h2, _, _ = layer_norm(mid, gain, shift)
    return mid, h2.astype(BF16)


def feed_forward(h2b, gyb, first, bias, second):
    pre = tdot(h2b, first) + bias
    phi = 0.5 * (1.0 + lax.erf(pre * 0.7071067811865476))
    act = (pre * phi).astype(BF16)
    slope = phi + pre * jnp.exp(-0.5 * pre * pre) * 0.3989422804014327
    dpre = nt_dot(gyb, second) * slope
    dpreb = dpre.astype(BF16)
    dh2 = nt_dot(dpreb, first).astype(BF16)
    return act, dpreb, dh2, jnp.sum(dpre, axis=0, keepdims=True)[None]


def middle_backward(dh2, mid, gyb, weight, gain):
    gy = gyb.astype(F32)
    _, normed, inv = layer_norm(mid, gain, gain)
    dmid = gy + norm_back(dh2, normed, inv, gain)
    dmidb = dmid.astype(BF16)
    dctx = nt_dot(dmidb, weight).astype(BF16)
    sums = [
        jnp.sum(dmid, axis=0, keepdims=True),
        jnp.sum(dh2 * normed, axis=0, keepdims=True),
        jnp.sum(dh2, axis=0, keepdims=True),
        jnp.sum(gy, axis=0, keepdims=True),
    ]
    return dmid, dmidb, dctx, *sums


def input_backward(dh1, dmid, x, gain):
    _, normed, inv = layer_norm(x.astype(F32), gain, gain)
    grad_x = dmid + norm_back(dh1, normed, inv, gain)
    return (
        grad_x,
        jnp.sum(dh1 * normed, axis=0, keepdims=True),
        jnp.sum(dh1, axis=0, keepdims=True),
    )


def run_kernel(fn, steps, cut_ins, whole_ins, outs, name, flops):
    def spec(shape, cut):
        block = (shape[0] // steps,) + tuple(shape[1:]) if cut else tuple(shape)
        zeros = (0,) * (len(shape) - 1)
        return pl.BlockSpec(block, (lambda i: (i,) + zeros) if cut else (lambda i: (0,) + zeros))

    count = len(cut_ins) + len(whole_ins)

    def kernel(*refs):
        values = fn(*[r[...] for r in refs[:count]])
        for ref, value in zip(refs[count:], values):
            ref[...] = value

    moved = sum(a.size * a.dtype.itemsize for a in (*cut_ins, *whole_ins))
    moved += sum(math.prod(s) * jnp.dtype(d).itemsize for s, d in outs)
    return pl.pallas_call(
        kernel,
        grid=(steps,),
        in_specs=[spec(a.shape, True) for a in cut_ins] + [spec(a.shape, False) for a in whole_ins],
        out_specs=[spec(s, True) for s, _ in outs],
        out_shape=[jax.ShapeDtypeStruct(s, d) for s, d in outs],
        compiler_params=pltpu.CompilerParams(
            dimension_semantics=("arbitrary",), vmem_limit_bytes=VMEM_LIMIT
        ),
        cost_estimate=pl.CostEstimate(flops=flops, bytes_accessed=moved, transcendentals=0),
        name=name,
    )(*cut_ins, *whole_ins)


def swap(value, axis):
    return lax.ppermute(value, axis, SWAP)


def pick(value, index, axis=0):
    return lax.dynamic_index_in_dim(value, index, axis, keepdims=False)


def ordered(own, other, index, axis):
    return jnp.where(
        index == 0, jnp.stack([own, other], axis), jnp.stack([other, own], axis)
    )


def gather_pair(value, axis_name, index, axis):
    return ordered(value, swap(value, axis_name), index, axis)


def trade_pair(value, axis_name, index, axis):
    other = swap(pick(value, 1 - index, axis), axis_name)
    return ordered(pick(value, index, axis), other, index, axis)


def ring_gather(block, ring, place, rest_sizes):
    z, x = place
    step = tuple((i, (i + 1) % ring) for i in range(ring))
    starts = [sum(rest_sizes[:n]) for n in range(len(rest_sizes))]
    outs = [jnp.zeros((ring, 2, n, block.shape[1]), block.dtype) for n in rest_sizes]
    for s in range(ring):
        if s:
            block = lax.ppermute(block, "z", step)
        pair = gather_pair(block, "x", x, 0)
        at = lax.rem(z - s + ring, ring)
        for n, (start, size) in enumerate(zip(starts, rest_sizes)):
            outs[n] = lax.dynamic_update_slice(
                outs[n], pair[None, :, start : start + size], (at, 0, 0, 0)
            )
    return outs


def ring_scatter(grad, ring, place):
    z, x = place
    step = tuple((i, (i + 1) % ring) for i in range(ring))
    cut = grad.reshape(ring, 2, -1, grad.shape[-1])
    own = pick(cut, x, 1)
    other = swap(pick(cut, 1 - x, 1), "x")
    total = None
    for s in range(1, ring + 1):
        at = lax.rem(z - s + ring, ring)
        term = pick(own, at).astype(F32) + pick(other, at).astype(F32)
        total = term if total is None else total + term
        if s < ring:
            total = lax.ppermute(total.astype(BF16), "z", step).astype(F32)
    return total


def on_device_split(
    ring,
    inputs,
    micro_live,
    ln1_gain,
    ln1_shift,
    w_q,
    b_q,
    w_k,
    w_v,
    b_v,
    w_o,
    b_o,
    ln2_gain,
    ln2_shift,
    w_fc1,
    b_fc1,
    w_fc2,
    b_fc2,
    grad_out,
):
    z, x, c, y = (lax.axis_index(a) for a in ("z", "x", "c", "y"))
    place = (z, x)
    me = 2 * c + y
    slots, count, width = inputs.shape
    rows = slots * count
    shard = w_q.shape[0]
    units = w_fc2.shape[0]
    groups = 2 * ring
    part = width // 4
    wide = w_fc1.shape[1] // 4
    all_slots, frames = 2 * slots, 2 * count
    all_rows = all_slots * frames

    def gather_rows(value):
        both = gather_pair(value, "y", y, 1).reshape(slots, frames, width)
        return gather_pair(both, "c", c, 0).reshape(all_rows, width)

    def scatter_rows(value):
        cut = value.reshape(2, slots, 2, count, width)
        own = pick(cut, c).astype(F32)
        half = own + swap(pick(cut, 1 - c), "c").astype(F32)
        other = swap(pick(half, 1 - y, 1).astype(BF16), "y").astype(F32)
        return (pick(half, y, 1) + other).reshape(rows, width)

    def trade_four(value):
        cut = value.reshape(2, 2, *value.shape[1:])
        return trade_pair(trade_pair(cut, "y", y, 1), "c", c, 0).reshape(value.shape)

    columns = jnp.stack([w_q, w_k, w_v], 1).reshape(shard, 3, 4, part)
    columns = columns.transpose(2, 0, 1, 3).reshape(4, shard, 3 * part)
    vector_rows = jnp.stack([ln1_gain, ln1_shift, b_q, b_v, b_o, ln2_gain, ln2_shift, b_fc2])
    vector_rows = jnp.pad(vector_rows, ((0, 8), (0, 3 * part - shard)))
    vector_rows = jnp.broadcast_to(vector_rows, (4, 16, 3 * part))
    first = trade_four(jnp.concatenate([columns, vector_rows], axis=1))
    vectors = first[:, shard : shard + 8, :shard].transpose(1, 0, 2).reshape(8, 4 * shard)
    vectors = jnp.pad(vectors, ((0, 0), (0, 3 * part - 4 * shard)))
    units_row = jnp.pad(b_fc1.reshape(1, units), ((0, 7), (0, 3 * part - units)))
    block = jnp.concatenate([first[:, :shard].reshape(4 * shard, 3 * part), vectors, units_row])
    x_all = gather_rows(inputs)
    w_qkv, vectors = ring_gather(block, ring, place, (4 * shard, 16))
    w_qkv = w_qkv.reshape(width, 3 * part)
    vectors = vectors.reshape(groups, 16, 3 * part)
    named = vectors[:, :8, : 4 * shard].transpose(1, 0, 2).reshape(8, 1, width).astype(F32)
    g1, c1, bq, bv, bo, g2, c2, bf2 = [named[n] for n in range(8)]
    bf1 = vectors[:, 8, :units].reshape(1, wide).astype(F32)

    columns = w_fc1.reshape(shard, groups, 4, units).transpose(2, 0, 1, 3).reshape(4, shard, wide)
    block = trade_four(columns).reshape(4 * shard, wide)
    wo_block, wf1 = ring_gather(
        jnp.concatenate([w_o, block]), ring, place, (shard, 4 * shard)
    )
    wf1 = wf1.reshape(width, wide)
    wo = gather_pair(wo_block.reshape(groups, shard, width), "y", y, 1)
    wo = gather_pair(wo, "c", c, 1).reshape(width, width)
    live = micro_live.astype(F32)[:, None, None]
    gy_own = (live * grad_out.astype(F32)).astype(BF16)
    gy_all = gather_rows(gy_own)
    gy_own = gy_own.reshape(rows, width)
    (wf2,) = ring_gather(w_fc2, ring, place, (units,))
    wf2 = wf2.reshape(wide, width)

    bias = jnp.concatenate(
        [
            lax.dynamic_slice(bq, (0, me * part), (1, part)),
            jnp.zeros((1, part), F32),
            lax.dynamic_slice(bv, (0, me * part), (1, part)),
        ],
        axis=1,
    )
    steps = 2
    heads = part // HD
    h1b, q, k, v, probs, ctxb = run_kernel(
        functools.partial(attention_forward, all_slots // steps),
        steps,
        (x_all,),
        (g1, c1, w_qkv, bias),
        [
            ((all_rows, width), BF16),
            ((all_rows, part), BF16),
            ((all_rows, part), BF16),
            ((all_rows, part), BF16),
            ((all_slots * heads, frames, frames), F32),
            ((all_rows, part), BF16),
        ],
        "attention_forward",
        2 * all_rows * part * (3 * width + 2 * frames),
    )

    def to_rows(value):
        cut = value.reshape(2, slots, 2, count, part)
        cut = trade_pair(trade_pair(cut, "y", y, 2), "c", c, 0)
        return cut.transpose(1, 3, 0, 2, 4).reshape(rows, width)

    def to_heads(value):
        cut = value.reshape(slots, count, 2, 2, part).transpose(2, 0, 3, 1, 4)
        return trade_pair(trade_pair(cut, "y", y, 2), "c", c, 0).reshape(all_rows, part)

    ctx_own = to_rows(ctxb)
    x_own = inputs.reshape(rows, width)
    mid, h2_own = run_kernel(
        out_projection,
        1,
        (x_own, ctx_own),
        (wo, bo, g2, c2),
        [((rows, width), F32), ((rows, width), BF16)],
        "out_projection",
        2 * rows * width * width,
    )
    h2_all = gather_rows(h2_own.reshape(slots, count, width))
    act, dpreb, dh2_part, dpre_sum = run_kernel(
        feed_forward,
        steps,
        (h2_all, gy_all),
        (wf1, bf1, wf2),
        [
            ((all_rows, wide), BF16),
            ((all_rows, wide), BF16),
            ((all_rows, width), BF16),
            ((steps, 1, wide), F32),
        ],
        "feed_forward",
        6 * all_rows * width * wide,
    )
    dh2 = scatter_rows(dh2_part)
    grad_fc2 = ring_scatter(tdot(act.T, gy_all).astype(BF16), ring, place)
    grad_fc1 = ring_scatter(tdot(h2_all.T, dpreb).astype(BF16), ring, place)
    out_part = scatter_rows(tdot(act, wf2).astype(BF16))
    result = live * (mid + out_part + bf2).reshape(slots, count, width)
    result = result.astype(BF16)

    dmid, dmidb, dctx_own, bo_sum, g2_sum, c2_sum, bf2_sum = run_kernel(
        middle_backward,
        1,
        (dh2, mid, gy_own),
        (wo, g2),
        [((rows, width), F32), ((rows, width), BF16), ((rows, width), BF16)]
        + [((1, width), F32)] * 4,
        "middle_backward",
        2 * rows * width * width,
    )
    dctx = to_heads(dctx_own)
    dqkv, dh1_part, bq_sum, bv_sum = run_kernel(
        functools.partial(attention_backward, all_slots // steps),
        steps,
        (dctx, q, k, v, probs),
        (w_qkv,),
        [
            ((all_rows, 3 * part), BF16),
            ((all_rows, width), BF16),
            ((steps, 1, part), F32),
            ((steps, 1, part), F32),
        ],
        "attention_backward",
        2 * all_rows * part * (3 * width + 4 * frames),
    )
    grad_qkv = ring_scatter(tdot(h1b.T, dqkv).astype(BF16), ring, place)
    dh1 = scatter_rows(dh1_part)
    grad_x, g1_sum, c1_sum = run_kernel(
        input_backward,
        1,
        (dh1, dmid, x_own),
        (g1,),
        [((rows, width), F32), ((1, width), F32), ((1, width), F32)],
        "input_backward",
        rows * width,
    )

    cut = tdot(ctx_own.T, dmidb).astype(BF16).reshape(groups, 2, 2, shard, width)
    half = pick(cut, c, 1).astype(F32) + swap(pick(cut, 1 - c, 1), "c").astype(F32)
    quarter = pick(half, y, 1) + swap(pick(half, 1 - y, 1).astype(BF16), "y").astype(F32)
    grad_o = ring_scatter(quarter.astype(BF16).reshape(groups * shard, width), ring, place)

    back = grad_fc1.astype(BF16).reshape(4, shard, groups, units)
    grad_fc1 = trade_four(back).transpose(1, 2, 0, 3).reshape(shard, 4 * wide).astype(F32)
    back = trade_four(grad_qkv.astype(BF16).reshape(4, shard, 3 * part)).astype(F32)
    grad_q, grad_k, grad_v = [
        back[:, :, n * part : (n + 1) * part].transpose(1, 0, 2).reshape(shard, width)
        for n in range(3)
    ]

    mine = (jnp.arange(4) == me).astype(F32)[:, None]
    spread = lambda value: mine * jnp.pad(value, ((0, 0), (0, width - value.shape[1])))
    packed = jnp.concatenate(
        [
            g1_sum,
            c1_sum,
            bo_sum,
            g2_sum,
            c2_sum,
            bf2_sum,
            spread(jnp.sum(dpre_sum, axis=0)),
            spread(jnp.sum(bq_sum, axis=0)),
            spread(jnp.sum(bv_sum, axis=0)),
            jnp.zeros((6, width), F32),
        ]
    )
    for axis in ("c", "y", "x"):
        packed = packed + swap(packed, axis)
    hop = 1
    while hop < ring:
        packed = packed + lax.ppermute(packed, "z", tuple((i, i ^ hop) for i in range(ring)))
        hop *= 2
    spot = (2 * z + x) * 4 + me
    own = lax.dynamic_slice(packed, (0, spot * shard), (6, shard))
    grad_bf1 = lax.dynamic_slice(packed, (6 + me, (2 * z + x) * units), (1, units))[0]
    per_part = part // shard
    head_row, head_at = spot // per_part, lax.rem(spot, per_part) * shard
    grad_bq = lax.dynamic_slice(packed, (10 + head_row, head_at), (1, shard))[0]
    grad_bv = lax.dynamic_slice(packed, (14 + head_row, head_at), (1, shard))[0]
    return (
        result,
        grad_x.reshape(slots, count, width),
        own[0],
        own[1],
        grad_q,
        grad_bq,
        grad_k,
        grad_v,
        grad_bv,
        grad_o,
        own[2],
        own[3],
        own[4],
        grad_fc1,
        grad_bf1,
        grad_fc2,
        own[5],
    )


def solution(mesh):
    clips, seqs = mesh.shape["clip"], mesh.shape["seq"]
    ring = clips // 4
    split = seqs == 2 and clips % 4 == 0 and ring & (ring - 1) == 0
    if split:
        names, both = ("z", "x", "c"), ("z", "x", "c", "y")
        grid = Mesh(mesh.devices.reshape(ring, 2, 2, 2), both)
        body, seq = functools.partial(on_device_split, ring), "y"
    else:
        names, both = ("clip",), ("clip", "seq")
        grid, body, seq = mesh, on_device_gathered, "seq"
    rows3 = P(names, seq, None)
    vector, matrix = P(both), P(both, None)
    in_specs = (
        rows3, P(names), vector, vector, matrix, vector, matrix, matrix, vector, matrix,
        vector, vector, vector, matrix, vector, matrix, vector, rows3,
    )
    out_specs = (
        rows3, rows3, vector, vector, matrix, vector, matrix, matrix, vector, matrix,
        vector, vector, vector, matrix, vector, matrix, vector,
    )
    return jax.shard_map(
        body, mesh=grid, in_specs=in_specs, out_specs=out_specs, check_vma=False
    )
```

```python
import functools
import math

import jax
import jax.numpy as jnp
from jax import lax
from jax.experimental import pallas as pl
from jax.experimental.pallas import tpu as pltpu
from jax.sharding import Mesh
from jax.sharding import PartitionSpec as P

HEADS = 12
HD = 64


norm_eps = 1e-05


def layer_norm(values, gain, shift):
    center = values - jnp.mean(values, axis=-1, keepdims=True)
    inv_std = lax.rsqrt(jnp.mean(center * center, axis=-1, keepdims=True) + norm_eps)
    normed = center * inv_std
    return (normed * gain + shift, normed, inv_std)


def norm_back(grad_in, normed, inv_std, gain):
    scaled = grad_in * gain
    inner = (
        scaled
        - jnp.mean(scaled, axis=-1, keepdims=True)
        - normed * jnp.mean(scaled * normed, axis=-1, keepdims=True)
    )
    return inv_std * inner


def gelu_slope(pre):
    return (
        0.5 * (1.0 + lax.erf(pre * 0.7071067811865476))
        + pre * jnp.exp(-0.5 * pre * pre) * 0.3989422804014327
    )


def tdot(left, right):
    return jnp.dot(left, right, preferred_element_type=jnp.float32)


def on_device_gathered(
    inputs,
    micro_live,
    ln1_gain,
    ln1_shift,
    w_q,
    b_q,
    w_k,
    w_v,
    b_v,
    w_o,
    b_o,
    ln2_gain,
    ln2_shift,
    w_fc1,
    b_fc1,
    w_fc2,
    b_fc2,
    grad_out,
):
    f32 = jnp.float32
    bf16 = jnp.bfloat16
    scale = 1.0 / math.sqrt(HD)
    params = (
        lax.all_gather(ln1_gain, ("clip", "seq"), axis=0, tiled=True),
        lax.all_gather(ln1_shift, ("clip", "seq"), axis=0, tiled=True),
        lax.all_gather(w_q, ("clip", "seq"), axis=0, tiled=True),
        lax.all_gather(b_q, ("clip", "seq"), axis=0, tiled=True),
        lax.all_gather(w_k, ("clip", "seq"), axis=0, tiled=True),
        lax.all_gather(w_v, ("clip", "seq"), axis=0, tiled=True),
        lax.all_gather(b_v, ("clip", "seq"), axis=0, tiled=True),
        lax.all_gather(w_o, ("clip", "seq"), axis=0, tiled=True),
        lax.all_gather(b_o, ("clip", "seq"), axis=0, tiled=True),
        lax.all_gather(ln2_gain, ("clip", "seq"), axis=0, tiled=True),
        lax.all_gather(ln2_shift, ("clip", "seq"), axis=0, tiled=True),
        lax.all_gather(w_fc1, ("clip", "seq"), axis=0, tiled=True),
        lax.all_gather(b_fc1, ("clip", "seq"), axis=0, tiled=True),
        lax.all_gather(w_fc2, ("clip", "seq"), axis=0, tiled=True),
        lax.all_gather(b_fc2, ("clip", "seq"), axis=0, tiled=True),
    )
    g1, c1, wq, bq, wk, wv, bv, wo, bo, g2, c2, wf1, bf1, wf2, bf2 = params
    slots, count, width = inputs.shape
    total_rows = slots * count
    live = micro_live.astype(f32)[:, None, None]
    x = inputs.astype(f32)
    h1, n1, r1 = layer_norm(x, g1.astype(f32), c1.astype(f32))
    h1b = h1.astype(bf16).reshape(total_rows, width)
    qb = (tdot(h1b, wq) + bq.astype(f32)).astype(bf16).reshape(slots, count, width)
    kb = tdot(h1b, wk).astype(bf16).reshape(slots, count, width)
    vb = (tdot(h1b, wv) + bv.astype(f32)).astype(bf16).reshape(slots, count, width)
    key_all, value_all = (
        lax.all_gather(kb, "seq", axis=1, tiled=True),
        lax.all_gather(vb, "seq", axis=1, tiled=True),
    )
    frames = key_all.shape[1]
    q4 = qb.reshape(slots, count, HEADS, HD)
    k4 = key_all.reshape(slots, frames, HEADS, HD)
    v4 = value_all.reshape(slots, frames, HEADS, HD)
    scores = jnp.einsum("sqhd,skhd->shqk", q4, k4, preferred_element_type=f32) * scale
    peak = jnp.max(scores, axis=-1, keepdims=True)
    lse = peak + jnp.log(jnp.sum(jnp.exp(scores - peak), axis=-1, keepdims=True))
    probs = jnp.exp(scores - lse)
    pb = probs.astype(bf16)
    ctxb = (
        jnp.einsum("shqk,skhd->sqhd", pb, v4, preferred_element_type=f32)
        .reshape(total_rows, width)
        .astype(bf16)
    )
    mid = x + tdot(ctxb, wo).reshape(slots, count, width) + bo.astype(f32)
    h2, n2, r2 = layer_norm(mid, g2.astype(f32), c2.astype(f32))
    h2b = h2.astype(bf16).reshape(total_rows, width)
    pre = tdot(h2b, wf1) + bf1.astype(f32)
    actb = jax.nn.gelu(pre, approximate=False).astype(bf16)
    result = (live * (mid + tdot(actb, wf2).reshape(slots, count, width) + bf2.astype(f32))).astype(
        bf16
    )
    gy = live * grad_out.astype(f32)
    gyb = gy.astype(bf16).reshape(total_rows, width)
    dpre = tdot(gyb, wf2.T) * gelu_slope(pre)
    dpreb = dpre.astype(bf16)
    dh2 = tdot(dpreb, wf1.T).reshape(slots, count, width)
    dmid = gy + norm_back(dh2, n2, r2, g2.astype(f32))
    dmidb = dmid.astype(bf16).reshape(total_rows, width)
    dctxb = tdot(dmidb, wo.T).astype(bf16).reshape(slots, count, width)
    dc4 = dctxb.reshape(slots, count, HEADS, HD)
    dprob = jnp.einsum("sqhd,skhd->shqk", dc4, v4, preferred_element_type=f32)
    delta = jnp.sum(probs * dprob, axis=-1, keepdims=True)
    dsb = (probs * (dprob - delta) * scale).astype(bf16)
    dq = jnp.einsum("shqk,skhd->sqhd", dsb, k4, preferred_element_type=f32).reshape(
        total_rows, width
    )
    key_terms = jnp.einsum("shqk,sqhd->skhd", dsb, q4, preferred_element_type=f32).reshape(
        slots, frames, width
    )
    value_terms = jnp.einsum("shqk,sqhd->skhd", pb, dc4, preferred_element_type=f32).reshape(
        slots, frames, width
    )
    dk, dv = (
        lax.psum_scatter(key_terms, "seq", scatter_dimension=1, tiled=True),
        lax.psum_scatter(value_terms, "seq", scatter_dimension=1, tiled=True),
    )
    dk = dk.reshape(total_rows, width)
    dv = dv.reshape(total_rows, width)
    dqb = dq.astype(bf16)
    dkb = dk.astype(bf16)
    dvb = dv.astype(bf16)
    dh1 = (tdot(dqb, wq.T) + tdot(dkb, wk.T) + tdot(dvb, wv.T)).reshape(slots, count, width)
    grad_x = dmid + norm_back(dh1, n1, r1, g1.astype(f32))
    first_cols = h1b.T
    ctx_cols = ctxb.T
    second_cols = h2b.T
    stacked = lax.psum_scatter(
        jnp.concatenate(
            [
                tdot(first_cols, dqb),
                tdot(first_cols, dkb),
                tdot(first_cols, dvb),
                tdot(ctx_cols, dmidb),
                tdot(second_cols, dpreb),
            ],
            axis=1,
        ),
        ("clip", "seq"),
        scatter_dimension=0,
        tiled=True,
    )
    act_cols = actb.T
    grad_fc2 = lax.psum_scatter(
        tdot(act_cols, gyb), ("clip", "seq"), scatter_dimension=0, tiled=True
    )
    grad_q = stacked[:, 0:width]
    grad_k = stacked[:, width : 2 * width]
    grad_v = stacked[:, 2 * width : 3 * width]
    grad_o = stacked[:, 3 * width : 4 * width]
    grad_fc1 = stacked[:, 4 * width :]
    n1f = n1.reshape(total_rows, width)
    n2f = n2.reshape(total_rows, width)
    dh1f = dh1.reshape(total_rows, width)
    dh2f = dh2.reshape(total_rows, width)
    dmidf = dmid.reshape(total_rows, width)
    gyf = gy.reshape(total_rows, width)
    vectors = (
        lax.psum_scatter(
            jnp.sum(dh1f * n1f, axis=0), ("clip", "seq"), scatter_dimension=0, tiled=True
        ),
        lax.psum_scatter(jnp.sum(dh1f, axis=0), ("clip", "seq"), scatter_dimension=0, tiled=True),
        lax.psum_scatter(jnp.sum(dq, axis=0), ("clip", "seq"), scatter_dimension=0, tiled=True),
        lax.psum_scatter(jnp.sum(dv, axis=0), ("clip", "seq"), scatter_dimension=0, tiled=True),
        lax.psum_scatter(jnp.sum(dmidf, axis=0), ("clip", "seq"), scatter_dimension=0, tiled=True),
        lax.psum_scatter(
            jnp.sum(dh2f * n2f, axis=0), ("clip", "seq"), scatter_dimension=0, tiled=True
        ),
        lax.psum_scatter(jnp.sum(dh2f, axis=0), ("clip", "seq"), scatter_dimension=0, tiled=True),
        lax.psum_scatter(jnp.sum(dpre, axis=0), ("clip", "seq"), scatter_dimension=0, tiled=True),
        lax.psum_scatter(jnp.sum(gyf, axis=0), ("clip", "seq"), scatter_dimension=0, tiled=True),
    )
    return (
        result,
        grad_x,
        vectors[0],
        vectors[1],
        grad_q,
        vectors[2],
        grad_k,
        grad_v,
        vectors[3],
        grad_o,
        vectors[4],
        vectors[5],
        vectors[6],
        grad_fc1,
        vectors[7],
        grad_fc2,
        vectors[8],
    )


F32 = jnp.float32
BF16 = jnp.bfloat16
SCALE = 1.0 / math.sqrt(HD)
SWAP = ((0, 1), (1, 0))
VMEM_LIMIT = 56 * 1024 * 1024
G1, C1, BQ, BV, BO, G2, C2, BF2, BF1 = range(9)


def nt_dot(left, right):
    return lax.dot_general(left, right, (((1,), (1,)), ((), ())), preferred_element_type=F32)


def tn_dot(left, right):
    return lax.dot_general(left, right, (((0,), (0,)), ((), ())), preferred_element_type=F32)


def row_of(named, n):
    return named[n : n + 1, :].astype(F32)


def head_masks(rows, width):
    lanes = lax.broadcasted_iota(jnp.int32, (rows, width), 1)
    return [
        jnp.where((lanes >= h * HD) & (lanes < (h + 1) * HD), 1.0, 0.0).astype(F32)
        for h in range(width // HD)
    ]


def quarter_of(row, me, part):
    total = None
    for t in range(4):
        piece = jnp.where(me == t, 1.0, 0.0).astype(F32) * row[:, t * part : (t + 1) * part]
        total = piece if total is None else total + piece
    return total


def pack_columns(spot, w_q, w_k, w_v, vectors, own, along_y, along_c):
    me = spot[4]
    part = own.shape[1] // 3
    mats = [r[...].astype(F32) for r in (w_q, w_k, w_v)]
    pads = vectors[...].astype(F32)

    def piece(t):
        columns = jnp.concatenate([m[:, t * part : (t + 1) * part] for m in mats], axis=1)
        return jnp.concatenate([columns, pads], axis=0).astype(BF16)

    for t in range(4):
        value = piece(t)
        rel = t ^ me

        @pl.when(rel == 0)
        def _():
            own[...] = value

        @pl.when(rel == 2)
        def _():
            along_c[...] = value

        @pl.when(rel == 1)
        def _():
            along_y[0] = value

        @pl.when(rel == 3)
        def _():
            along_y[1] = value


def clip_rows(base, s, count, rows):
    return (
        pl.ds(pl.multiple_of(base + s * count, count), count),
        pl.ds(pl.multiple_of(base + rows + s * count, count), count),
    )


def attention_forward(
    spot, x0, x1, x2, x3, named, weight, h1_ref, q_ref, k_ref, v_ref, probs_ref, own, along_y, along_c, ctx
):
    slots, count, width = x0.shape
    rows = slots * count
    part = q_ref.shape[1]
    names = named[...]
    gain, shift = row_of(names, G1), row_of(names, C1)
    for n, x in enumerate((x0, x1, x2, x3)):
        h1, _, _ = layer_norm(x[...].reshape(rows, width).astype(F32), gain, shift)
        h1_ref[n * rows : (n + 1) * rows, :] = h1.astype(BF16)
    me = spot[4]
    qkv = tdot(h1_ref[...], weight[...])
    q_ref[...] = (qkv[:, :part] + quarter_of(row_of(names, BQ), me, part)).astype(BF16)
    k_ref[...] = qkv[:, part : 2 * part].astype(BF16)
    v_ref[...] = (qkv[:, 2 * part :] + quarter_of(row_of(names, BV), me, part)).astype(BF16)
    masks32 = head_masks(2 * count, part)
    masks = [m.astype(BF16) for m in masks32]

    def one(pair, carry):
        base = pair * 2 * rows
        for s in range(slots):
            low, high = clip_rows(base, s, count, rows)
            qs, ks, vs = [
                jnp.concatenate([r[low, :], r[high, :]], axis=0) for r in (q_ref, k_ref, v_ref)
            ]
            total = None
            for h, (mask, mask32) in enumerate(zip(masks, masks32)):
                scores = nt_dot(qs * mask, ks) * SCALE
                peak = jnp.max(scores, axis=-1, keepdims=True)
                lse = peak + jnp.log(jnp.sum(jnp.exp(scores - peak), axis=-1, keepdims=True))
                probs = jnp.exp(scores - lse)
                probs_ref[(pair * slots + s) * len(masks) + h] = probs
                term = tdot(probs.astype(BF16), vs) * mask32
                total = term if total is None else total + term
            totalb = total.astype(BF16)
            ctx[low, :] = totalb[:count]
            ctx[high, :] = totalb[count:]
        return carry

    lax.fori_loop(0, 2, one, 0)
    own[...] = ctx[0:rows, :]
    along_y[0] = ctx[rows : 2 * rows, :]
    along_c[...] = ctx[2 * rows : 3 * rows, :]
    along_y[1] = ctx[3 * rows : 4 * rows, :]


def attention_backward(
    spot, d0, d1, d2, d3, q_ref, k_ref, v_ref, probs_ref, weight, h1_ref,
    dh_own, dh_c, bq_ref, bv_ref, keep, send_far, send_near, dctx, grads
):
    rows = d0.shape[0]
    part = q_ref.shape[1]
    count = probs_ref.shape[1] // 2
    slots = rows // count
    for n, d in enumerate((d0, d1, d2, d3)):
        dctx[n * rows : (n + 1) * rows, :] = d[...]
    masks32 = head_masks(2 * count, part)
    masks = [m.astype(BF16) for m in masks32]
    bq_ref[...] = jnp.zeros(bq_ref.shape, F32)
    bv_ref[...] = jnp.zeros(bv_ref.shape, F32)

    def one(pair, carry):
        base = pair * 2 * rows
        for s in range(slots):
            low, high = clip_rows(base, s, count, rows)
            ds_, qs, ks, vs = [
                jnp.concatenate([r[low, :], r[high, :]], axis=0)
                for r in (dctx, q_ref, k_ref, v_ref)
            ]
            dq = dk = dv = None
            for h, (mask, mask32) in enumerate(zip(masks, masks32)):
                p = probs_ref[(pair * slots + s) * len(masks) + h]
                dprob = nt_dot(ds_ * mask, vs)
                delta = jnp.sum(p * dprob, axis=-1, keepdims=True)
                dsb = (p * (dprob - delta) * SCALE).astype(BF16)
                tq = tdot(dsb, ks) * mask32
                tk = tn_dot(dsb, qs) * mask32
                tv = tn_dot(p.astype(BF16), ds_) * mask32
                dq = tq if dq is None else dq + tq
                dk = tk if dk is None else dk + tk
                dv = tv if dv is None else dv + tv
            bq_ref[...] += jnp.sum(dq, axis=0, keepdims=True)
            bv_ref[...] += jnp.sum(dv, axis=0, keepdims=True)
            all_three = jnp.concatenate([dq, dk, dv], axis=1).astype(BF16)
            grads[low, :] = all_three[:count]
            grads[high, :] = all_three[count:]
        return carry

    lax.fori_loop(0, 2, one, 0)
    place_blocks(spot, tn_dot(h1_ref[...], grads[...]), keep, (send_near, send_far))
    dh1 = nt_dot(grads[...], weight[...]).astype(BF16)
    for n in range(2):
        dh_own[n] = dh1[n * rows : (n + 1) * rows]
        dh_c[n] = dh1[(2 + n) * rows : (3 + n) * rows]


def place_blocks(spot, grad, keep, sends):
    z, x = spot[0], spot[1]
    size = keep.shape[1]
    held = keep.shape[0] // len(sends)
    for zz in range(keep.shape[0]):
        pair = [grad[(2 * zz + n) * size : (2 * zz + n + 1) * size] for n in range(2)]
        far = zz ^ z
        first = x == 0
        keep[far] = jnp.where(first, pair[0], pair[1]).astype(BF16)
        other = jnp.where(first, pair[1], pair[0]).astype(BF16)
        for n, ref in enumerate(sends):
            if len(sends) == 1:
                ref[far] = other
            else:

                @pl.when((far >= n * held) & (far < (n + 1) * held))
                def _():
                    ref[far - n * held] = other


def out_projection(spot, x, c0, c1, c2, c3, weight, named, mid_ref, h2_ref):
    me = spot[4]
    names = named[...]
    total = x[...].astype(F32) + row_of(names, BO)
    for n, piece in enumerate((c0, c1, c2, c3)):
        total = total + tdot(piece[...], weight[me ^ n])
    mid_ref[...] = total
    h2, _, _ = layer_norm(total, row_of(names, G2), row_of(names, C2))
    h2_ref[...] = h2.astype(BF16)


def feed_forward(
    spot, a0, a1, a2, a3, g0, g1, g2, g3, first, second, named,
    h2_ref, gy_ref, act_ref, dpre_ref, dh_own, dh_c, sum_ref
):
    rows = a0.shape[0]
    for n, (a, g) in enumerate(((a0, g0), (a1, g1), (a2, g2), (a3, g3))):
        h2_ref[n * rows : (n + 1) * rows, :] = a[...]
        gy_ref[n * rows : (n + 1) * rows, :] = g[...]
    bias = row_of(named[...], BF1)
    sum_ref[...] = jnp.zeros(sum_ref.shape, F32)

    def one(pair, carry):
        block = pl.ds(pl.multiple_of(pair * 2 * rows, 2 * rows), 2 * rows)
        pre = tdot(h2_ref[block, :], first[...]) + bias
        phi = 0.5 * (1.0 + lax.erf(pre * 0.7071067811865476))
        act_ref[block, :] = (pre * phi).astype(BF16)
        slope = phi + pre * jnp.exp(-0.5 * pre * pre) * 0.3989422804014327
        dpre = nt_dot(gy_ref[block, :], second[...]) * slope
        dpreb = dpre.astype(BF16)
        dpre_ref[block, :] = dpreb
        sum_ref[...] += jnp.sum(dpre, axis=0, keepdims=True)
        dh2 = nt_dot(dpreb, first[...]).astype(BF16)

        @pl.when(pair == 0)
        def _():
            dh_own[0] = dh2[:rows]
            dh_own[1] = dh2[rows:]

        @pl.when(pair == 1)
        def _():
            dh_c[0] = dh2[:rows]
            dh_c[1] = dh2[rows:]

        return carry

    lax.fori_loop(0, 2, one, 0)


def weight_gradient(spot, left, right, keep, send):
    place_blocks(spot, tn_dot(left[...], right[...]), keep, (send,))


def out_rows_part(spot, act, second, own, along_c):
    rows = own.shape[1]
    value = tdot(act[...], second[...]).astype(BF16)
    for n in range(2):
        own[n] = value[n * rows : (n + 1) * rows]
        along_c[n] = value[(2 + n) * rows : (3 + n) * rows]


def middle_backward(
    spot, d0, d1, d2, mid_ref, gy_ref, weight, named, dmid_ref, dmidb_ref, own, along_y, along_c, sums
):
    me = spot[4]
    gain = row_of(named[...], G2)
    gy = gy_ref[...].astype(F32)
    dh2 = d0[0].astype(F32) + d1[0].astype(F32) + d2[...].astype(F32)
    _, normed, inv = layer_norm(mid_ref[...], gain, gain)
    dmid = gy + norm_back(dh2, normed, inv, gain)
    dmidb = dmid.astype(BF16)
    dmid_ref[...] = dmid
    dmidb_ref[...] = dmidb
    parts = [nt_dot(dmidb, weight[me ^ n]).astype(BF16) for n in range(4)]
    own[...] = parts[0]
    along_y[0] = parts[1]
    along_c[...] = parts[2]
    along_y[1] = parts[3]
    for n, value in enumerate((dmid, dh2 * normed, dh2, gy)):
        sums[n : n + 1, :] = jnp.sum(value, axis=0, keepdims=True)
    sums[4:8, :] = jnp.zeros((4, gain.shape[1]), F32)


def out_gradient(spot, c0, c1, c2, c3, dmidb, own, along_c, held):
    z, x, c, y, me = [spot[n] for n in range(5)]
    size = held.shape[1]
    for n, piece in enumerate((c0, c1, c2, c3)):
        value = tn_dot(piece[...], dmidb[...])
        for b in range(8):
            held[b] = value[b * size : (b + 1) * size]
        far = (me ^ n) ^ z
        for cc, ref in enumerate((own, along_c)):
            for yy in range(2):
                pair = [held[4 * (x ^ xx) + 2 * (c ^ cc) + (y ^ yy)] for xx in range(2)]
                ref[yy, far] = jnp.concatenate(pair, axis=0).astype(BF16)


def input_backward(spot, d0, d1, d2, dmid, x, named, grad_ref, sums):
    gain = row_of(named[...], G1)
    dh1 = d0[0].astype(F32) + d1[0].astype(F32) + d2[...].astype(F32)
    _, normed, inv = layer_norm(x[...].astype(F32), gain, gain)
    grad_ref[...] = dmid[...] + norm_back(dh1, normed, inv, gain)
    sums[0:1, :] = jnp.sum(dh1 * normed, axis=0, keepdims=True)
    sums[1:2, :] = jnp.sum(dh1, axis=0, keepdims=True)
    sums[2:8, :] = jnp.zeros((6, gain.shape[1]), F32)


def run_kernel(body, spot, ins, outs, scratch, flops):
    moved = sum(a.size * a.dtype.itemsize for a in ins)
    moved += sum(math.prod(s) * jnp.dtype(d).itemsize for s, d in outs)
    return pl.pallas_call(
        body,
        in_specs=[pl.BlockSpec(memory_space=pltpu.SMEM)]
        + [pl.BlockSpec(memory_space=pltpu.VMEM)] * len(ins),
        out_specs=[pl.BlockSpec(memory_space=pltpu.VMEM)] * len(outs),
        out_shape=[jax.ShapeDtypeStruct(s, d) for s, d in outs],
        scratch_shapes=[pltpu.VMEM(s, d) for s, d in scratch],
        compiler_params=pltpu.CompilerParams(vmem_limit_bytes=VMEM_LIMIT),
        cost_estimate=pl.CostEstimate(flops=flops, bytes_accessed=moved, transcendentals=0),
        name=body.__name__,
    )(spot, *ins)


def swap(value, axis):
    return lax.ppermute(value, axis, SWAP)


def after(value, *others):
    return lax.optimization_barrier((value, *others))[0]


def pick(value, index, axis=0):
    return lax.dynamic_index_in_dim(value, index, axis, keepdims=False)


def ordered(own, other, index, axis):
    return jnp.where(index == 0, jnp.stack([own, other], axis), jnp.stack([other, own], axis))


def trade_pair(value, axis_name, index, axis):
    other = swap(pick(value, 1 - index, axis), axis_name)
    return ordered(pick(value, index, axis), other, index, axis)


def share_rows(value):
    over_y = swap(value, "y")
    return value, over_y, swap(value, "c"), swap(over_y, "c")


def trade_rows(own, along_y, along_c):
    over_y = swap(along_y, "y")
    return own, over_y[0], swap(along_c, "c"), swap(over_y[1], "c")


def sum_rows(own, along_c):
    over_c = swap(along_c, "c")
    other = (own[1].astype(F32) + over_c[1].astype(F32)).astype(BF16)
    return own, over_c, swap(other, "y")


def far_in_z(value, distance, ring):
    return lax.ppermute(value, "z", tuple((i, i ^ distance) for i in range(ring)))


def wide_gather(block, ring, place, sizes):
    z, x = place
    starts = [sum(sizes[:n]) for n in range(len(sizes))]
    outs = [jnp.zeros((2 * ring, n, block.shape[1]), block.dtype) for n in sizes]
    blocks = [block] + [far_in_z(block, d, ring) for d in range(1, ring)]
    for d, held in enumerate(blocks):
        for side, value in ((x, held), (1 - x, swap(held, "x"))):
            at = 2 * (z ^ d) + side
            for n, (start, size) in enumerate(zip(starts, sizes)):
                outs[n] = lax.dynamic_update_slice(
                    outs[n], value[None, start : start + size], (at, 0, 0)
                )
    return outs, blocks


def wide_sum(keep, others, ring):
    half = [keep[d].astype(F32) + others[d].astype(F32) for d in range(ring)]
    total = half[0]
    for d in range(ring - 1, 0, -1):
        total = total + far_in_z(half[d].astype(BF16), d, ring).astype(F32)
    return total


def on_device_split(
    ring,
    inputs,
    micro_live,
    ln1_gain,
    ln1_shift,
    w_q,
    b_q,
    w_k,
    w_v,
    b_v,
    w_o,
    b_o,
    ln2_gain,
    ln2_shift,
    w_fc1,
    b_fc1,
    w_fc2,
    b_fc2,
    grad_out,
):
    z, x, c, y = (lax.axis_index(a) for a in ("z", "x", "c", "y"))
    place = (z, x)
    me = 2 * c + y
    spot = jnp.stack([z, x, c, y, me]).astype(jnp.int32)
    slots, count, width = inputs.shape
    rows = slots * count
    shard = w_q.shape[0]
    units = w_fc2.shape[0]
    groups = 2 * ring
    part = width // 4
    wide = w_fc1.shape[1] // 4
    all_slots, frames = 2 * slots, 2 * count
    all_rows = all_slots * frames
    heads = part // HD

    def trade_four(value):
        cut = value.reshape(2, 2, *value.shape[1:])
        return trade_pair(trade_pair(cut, "y", y, 1), "c", c, 0).reshape(value.shape)

    vector_rows = jnp.stack([ln1_gain, ln1_shift, b_q, b_v, b_o, ln2_gain, ln2_shift, b_fc2])
    vector_rows = jnp.pad(vector_rows, ((0, 0), (0, 3 * part - shard)))
    piece = ((shard + 8, 3 * part), BF16)
    own, along_y, along_c = run_kernel(
        pack_columns,
        spot,
        (w_q, w_k, w_v, vector_rows),
        [piece, ((2, *piece[0]), BF16), piece],
        [],
        0,
    )
    pieces = trade_rows(own, along_y, along_c)
    first = jnp.zeros((4, *piece[0]), BF16)
    for n, value in enumerate(pieces):
        first = lax.dynamic_update_slice(first, value[None], (me ^ n, 0, 0))
    vectors = first[:, shard:, :shard].transpose(1, 0, 2).reshape(8, 4 * shard)
    vectors = jnp.pad(vectors, ((0, 0), (0, 3 * part - 4 * shard)))
    units_row = jnp.pad(b_fc1.reshape(1, units), ((0, 7), (0, 3 * part - units)))
    block = jnp.concatenate([first[:, :shard].reshape(4 * shard, 3 * part), vectors, units_row])
    x_all = share_rows(inputs)
    (w_qkv, vectors), arrived = wide_gather(block, ring, place, (4 * shard, 16))
    w_qkv = w_qkv.reshape(width, 3 * part)
    named = vectors[:, :, : 4 * shard].transpose(1, 0, 2).reshape(16, width)

    wo_block = after(w_o, arrived[1])
    (wo,), _ = wide_gather(wo_block, ring, place, (shard,))
    wo = ordered(wo, swap(wo, "y"), y, 1)
    wo = ordered(wo, swap(wo, "c"), c, 1).reshape(4, part, width)
    columns = w_fc1.reshape(shard, groups, 4, units).transpose(2, 0, 1, 3).reshape(4, shard, wide)
    block = trade_four(after(columns, pieces[1])).reshape(4 * shard, wide)
    block = after(jnp.concatenate([block, w_fc2]), arrived[ring - 1])
    (wf1, wf2), _ = wide_gather(block, ring, place, (4 * shard, units))
    wf1 = wf1.reshape(width, wide)
    wf2 = wf2.reshape(wide, width)
    live = micro_live.astype(F32)[:, None, None]
    gy_own = (live * grad_out.astype(F32)).astype(BF16).reshape(rows, width)
    gy_all = share_rows(after(gy_own, x_all[1]))

    row_part = ((all_rows, part), BF16)
    mine = [((rows, part), BF16), ((2, rows, part), BF16), ((rows, part), BF16)]
    h1b, q, k, v, probs, *ctx = run_kernel(
        attention_forward,
        spot,
        (*x_all, named, w_qkv),
        [
            ((all_rows, width), BF16),
            row_part,
            row_part,
            row_part,
            ((all_slots * heads, frames, frames), F32),
            *mine,
        ],
        [row_part],
        2 * all_rows * part * (3 * width + 2 * frames),
    )
    ctx = trade_rows(*ctx)
    x_own = inputs.reshape(rows, width)
    mid, h2_own = run_kernel(
        out_projection,
        spot,
        (x_own, *ctx, wo, named),
        [((rows, width), F32), ((rows, width), BF16)],
        [],
        2 * rows * width * width,
    )
    pair_rows = ((2, rows, width), BF16)
    h2_all, gy_rows, act, dpreb, dh2_own, dh2_c, dpre_sum = run_kernel(
        feed_forward,
        spot,
        (*share_rows(h2_own), *gy_all, wf1, wf2, named),
        [
            ((all_rows, width), BF16),
            ((all_rows, width), BF16),
            ((all_rows, wide), BF16),
            ((all_rows, wide), BF16),
            pair_rows,
            pair_rows,
            ((1, wide), F32),
        ],
        [],
        6 * all_rows * width * wide,
    )

    dh2 = sum_rows(dh2_own, dh2_c)

    def weight_grad(left, right, size):
        shape = ((ring, size, right.shape[1]), BF16)
        flops = 2 * left.shape[0] * left.shape[1] * right.shape[1]
        keep, send = run_kernel(weight_gradient, spot, (left, right), [shape, shape], [], flops)
        return wide_sum(keep, swap(send, "x"), ring)

    grad_fc2 = weight_grad(act, gy_rows, units)
    grad_fc1 = weight_grad(h2_all, dpreb, 4 * shard)
    dmid, dmidb, *dctx, sums2 = run_kernel(
        middle_backward,
        spot,
        (*dh2, mid, gy_own, wo, named),
        [((rows, width), F32), ((rows, width), BF16), *mine, ((8, width), F32)],
        [],
        2 * rows * width * width,
    )
    dctx = trade_rows(*dctx)
    out_own, out_c = run_kernel(
        out_rows_part,
        spot,
        (after(act, dh2[2]), wf2),
        [pair_rows, pair_rows],
        [],
        2 * all_rows * width * wide,
    )
    out_terms = sum_rows(out_own, out_c)
    ffn = out_terms[0][0].astype(F32) + out_terms[1][0].astype(F32) + out_terms[2].astype(F32)
    result = (mid + ffn + row_of(named, BF2)).reshape(slots, count, width)
    result = (live * result).astype(BF16)
    half_ring = ((ring // 2, 4 * shard, 3 * part), BF16)
    dh1_own, dh1_c, bq_sum, bv_sum, keep, send_far, send_near = run_kernel(
        attention_backward,
        spot,
        (*dctx, q, k, v, probs, w_qkv, h1b),
        [
            pair_rows,
            pair_rows,
            ((1, part), F32),
            ((1, part), F32),
            ((ring, 4 * shard, 3 * part), BF16),
            half_ring,
            half_ring,
        ],
        [row_part, ((all_rows, 3 * part), BF16)],
        2 * all_rows * part * (6 * width + 4 * frames),
    )
    far, near = swap(send_far, "x"), swap(send_near, "x")
    half = ring // 2
    others = [near[d] for d in range(half)] + [far[d] for d in range(half)]
    grad_qkv = wide_sum(keep, others, ring)
    dh1 = sum_rows(dh1_own, dh1_c)
    grad_x, sums1 = run_kernel(
        input_backward,
        spot,
        (*dh1, dmid, x_own, named),
        [((rows, width), F32), ((8, width), F32)],
        [],
        rows * width,
    )

    quarters = ((2, ring, 2 * shard, width), BF16)
    own, along_c = run_kernel(
        out_gradient,
        spot,
        (*ctx, dmidb),
        [quarters, quarters],
        [((8, shard, width), F32)],
        2 * rows * width * width,
    )
    over_c = swap(along_c, "c")
    over_y = swap((own[1].astype(F32) + over_c[1].astype(F32)).astype(BF16), "y")
    quarter = own[0].astype(F32) + over_c[0].astype(F32) + over_y.astype(F32)
    grad_o = wide_sum(quarter[:, :shard], swap(quarter[:, shard:].astype(BF16), "x"), ring)

    back = grad_fc1.astype(BF16).reshape(4, shard, groups, units)
    grad_fc1 = trade_four(back).transpose(1, 2, 0, 3).reshape(shard, 4 * wide).astype(F32)
    back = trade_four(grad_qkv.astype(BF16).reshape(4, shard, 3 * part)).astype(F32)
    grad_q, grad_k, grad_v = [
        back[:, :, n * part : (n + 1) * part].transpose(1, 0, 2).reshape(shard, width)
        for n in range(3)
    ]

    mine = (jnp.arange(4) == me).astype(F32)[:, None]
    spread = lambda value: mine * jnp.pad(value, ((0, 0), (0, width - value.shape[1])))
    packed = jnp.concatenate(
        [sums1[:2], sums2[:4], spread(dpre_sum), spread(bq_sum), spread(bv_sum), sums1[2:]]
    )
    for axis in ("c", "y", "x"):
        packed = packed + swap(packed, axis)
    packed = packed + sum(far_in_z(packed, d, ring) for d in range(1, ring))
    at = (2 * z + x) * 4 + me
    own = lax.dynamic_slice(packed, (0, at * shard), (6, shard))
    grad_bf1 = lax.dynamic_slice(packed, (6 + me, (2 * z + x) * units), (1, units))[0]
    per_part = part // shard
    head_row, head_at = at // per_part, lax.rem(at, per_part) * shard
    grad_bq = lax.dynamic_slice(packed, (10 + head_row, head_at), (1, shard))[0]
    grad_bv = lax.dynamic_slice(packed, (14 + head_row, head_at), (1, shard))[0]
    return (
        result,
        grad_x.reshape(slots, count, width),
        own[0],
        own[1],
        grad_q,
        grad_bq,
        grad_k,
        grad_v,
        grad_bv,
        grad_o,
        own[2],
        own[3],
        own[4],
        grad_fc1,
        grad_bf1,
        grad_fc2,
        own[5],
    )


def solution(mesh):
    clips, seqs = mesh.shape["clip"], mesh.shape["seq"]
    ring = clips // 4
    split = seqs == 2 and clips % 4 == 0 and ring & (ring - 1) == 0
    if split:
        names, both = ("z", "x", "c"), ("z", "x", "c", "y")
        grid = Mesh(mesh.devices.reshape(ring, 2, 2, 2), both)
        body, seq = functools.partial(on_device_split, ring), "y"
    else:
        names, both = ("clip",), ("clip", "seq")
        grid, body, seq = mesh, on_device_gathered, "seq"
    rows3 = P(names, seq, None)
    vector, matrix = P(both), P(both, None)
    in_specs = (
        rows3, P(names), vector, vector, matrix, vector, matrix, matrix, vector, matrix,
        vector, vector, vector, matrix, vector, matrix, vector, rows3,
    )
    out_specs = (
        rows3, rows3, vector, vector, matrix, vector, matrix, matrix, vector, matrix,
        vector, vector, vector, matrix, vector, matrix, vector,
    )
    return jax.shard_map(
        body, mesh=grid, in_specs=in_specs, out_specs=out_specs, check_vma=False
    )
```
